32 devices in a mesh: rep: 2 (over x), grp: 4 (over z), tp: 4 (over y, core).
Axes of the slice: x: 2, y: 2, z: 4, core: 2. Of those that a mesh axis runs over, the one named last changes fastest.
Arguments:
- queries: bfloat16 [512, 8192], P(('rep', 'grp'), 'tp'), parts along dimension 0, may hold values from -256 to 256
- newest_key_value: bfloat16 [512, 2, 1024], P(('rep', 'grp')), parts along dimension 0, may hold values from -6 to 6
- kv_pages: bfloat16 [128, 2, 128, 1024], P(('rep', 'grp', 'tp')), parts along dimension 0, may hold values from -8 to 8
- fetch_slots: int32 [8, 16, 2], P('rep', ('grp', 'tp')), parts along dimension 0, may hold values from -1 to 3, as said below
- block_table: int32 [512, 8], P(('rep', 'grp')), parts along dimension 0, may hold values from 0 to 31, as said below
- prefix_len: int32 [512], P(('rep', 'grp')), parts along dimension 0, may hold values from 2 to 1024
- out_weight: bfloat16 [8192, 8192], P('tp'), may hold values from -0.09375 to 0.09375
Outputs:
- attended: bfloat16 [512, 8192], P(('rep', 'grp'), 'tp'), parts along dimension 0
The draws below stay inside these ranges and needn't reach their ends.
There are 2 independent parts, one for each index of `rep`. The reference program is written for one: setup_inputs(seed, part) draws one part's arguments, and reference() takes and returns one part's arrays. A program takes and returns all parts, laid end to end along the dimension named above; an argument that names none is the same for every part. Nothing has to cross between parts.
Inputs may be any that keep to these rules, and one draw needn't show every extreme that they name: `fetch_slots`: entries of one (group, owner device) are distinct pages of that device's storage; each group takes at most 2 pages from one device, and in every draw some group takes exactly 2 from some device; -1 marks an unused entry, and used entries come first. `block_table`: every entry names a used entry of its group's fetch_slots; requests of a group share their first pages to a varying depth.
All inputs are finite; a program needn't handle non-finite values.
Results may differ from the reference program's by a relative error of at most 0.0057.
Values may be sent and summed in bfloat16 or wider, within the bound.
A program may use at most 128 MiB of HBM per device.

```python
import math
import jax
import jax.numpy as jnp
from jax import lax

D = 8192
QUERY_HEADS = 64
KEY_VALUE_HEADS = 8
HEAD_SIZE = 128
PAGE_TOKENS = 128
PAGE_LIST_LENGTH = 8
GROUP_PAGE_LIMIT = 2
REQ_GRP = 64
PAGES_DEV = 4
OWNERS = 16
TOTAL_PAGES = 64
SLOTS = 32
TOTAL_REQUESTS = 256
N_GRP = 4


def fetch_plan(key):
    base = jax.random.fold_in(key, 101)
    hot_owner = jax.random.randint(jax.random.fold_in(base, 1), (OWNERS,), 0, 4) == 0
    counts = jax.random.randint(jax.random.fold_in(base, 2), (N_GRP, OWNERS), 0, GROUP_PAGE_LIMIT + 1)
    counts = jnp.where(hot_owner[None, :], GROUP_PAGE_LIMIT, counts)
    forced = jnp.arange(N_GRP) * 7 % OWNERS
    counts = counts.at[jnp.arange(N_GRP), forced].set(GROUP_PAGE_LIMIT)
    perm_keys = jax.random.split(jax.random.fold_in(base, 3), N_GRP * OWNERS)
    perms = jax.vmap(lambda one_key: jax.random.permutation(one_key, PAGES_DEV)[:GROUP_PAGE_LIMIT])(perm_keys)
    perms = perms.reshape(N_GRP, OWNERS, GROUP_PAGE_LIMIT)
    filled = jnp.arange(GROUP_PAGE_LIMIT)[None, None, :] < counts[..., None]
    slots = jnp.where(filled, perms, -1).astype(jnp.int32)
    return (slots, filled)


def page_table(key):
    slots, filled = fetch_plan(key)
    flags = filled.reshape(N_GRP, SLOTS).astype(jnp.int32)
    order = jnp.argsort(1 - flags, axis=1, stable=True).astype(jnp.int32)
    count = jnp.sum(flags, axis=1)
    base = jax.random.fold_in(key, 202)
    group_of = jnp.arange(TOTAL_REQUESTS) // REQ_GRP
    shared_pick = jax.random.randint(jax.random.fold_in(base, 1), (N_GRP, PAGE_LIST_LENGTH), 0, 1 << 20) % count[:, None]
    own_pick = jax.random.randint(jax.random.fold_in(base, 2), (TOTAL_REQUESTS, PAGE_LIST_LENGTH), 0, 1 << 20) % count[group_of][:, None]
    depth = jax.random.randint(jax.random.fold_in(base, 3), (TOTAL_REQUESTS,), 0, PAGE_LIST_LENGTH + 1)
    pick = jnp.where(jnp.arange(PAGE_LIST_LENGTH)[None, :] < depth[:, None], shared_pick[group_of], own_pick)
    return jnp.take_along_axis(order[group_of], pick, axis=1).astype(jnp.int32)


def key_couples(key):
    first_index = jax.random.normal(jax.random.fold_in(key, 404), (TOTAL_PAGES, 2, KEY_VALUE_HEADS * HEAD_SIZE), jnp.float32)
    return jnp.clip(first_index, -6.0, 6.0)


def draw_fetch_slots(key, part):
    return fetch_plan(key)[0]


def draw_block_table(key, part):
    return page_table(key)


def draw_kv_pages(key, part):
    remaining_rows = jax.random.normal(jax.random.fold_in(key, 505), (TOTAL_PAGES, 2, PAGE_TOKENS, KEY_VALUE_HEADS * HEAD_SIZE), jnp.float32)
    remaining_rows = jnp.clip(remaining_rows, -6.0, 6.0)
    remaining_rows = remaining_rows.at[:, 0, 0:2].set(key_couples(key))
    return remaining_rows.astype(jnp.bfloat16)


def draw_queries(key, part):
    drawn = jax.random.normal(jax.random.fold_in(key, 606), (TOTAL_REQUESTS, QUERY_HEADS * HEAD_SIZE), jnp.float32)
    drawn = jnp.clip(drawn, -6.0, 6.0)
    return drawn.astype(jnp.bfloat16)


def place_ends(values, own_key, least, high):
    index_at = [jax.random.randint(jax.random.fold_in(own_key, axis), (), 0, length) for axis, length in enumerate(values.shape)]
    longest = values.shape.index(max(values.shape))
    neighbour = index_at[:longest] + [(index_at[longest] + 1) % values.shape[longest]] + index_at[longest + 1:]
    return values.at[tuple(index_at)].set(least).at[tuple(neighbour)].set(high)


def strengthened(result, stream_key, source, target, parts, factor):
    owner, partner = [(jnp.arange(result.shape[axis_at]) // (result.shape[axis_at] // parts)).reshape([-1 if axis == axis_at else 1 for axis in range(result.ndim)]) for axis_at in (source, target)]
    chosen = jax.random.permutation(stream_key, parts)[partner]
    strong = (owner == chosen) | (owner == (partner + parts // 2) % parts)
    return jnp.where(strong, factor * result, result)


def level_of(own_key, dims, shards, smallest, largest):
    level, own = 1.0, jax.random.fold_in(own_key, 6)
    for dim, parts in shards:
        steps = jnp.exp(jax.random.uniform(jax.random.fold_in(own, dim), (parts,), jnp.float32, smallest / len(shards), largest / len(shards)))
        level = level * jnp.repeat(steps, dims[dim] // parts).reshape([-1 if axis == dim else 1 for axis in range(len(dims))])
    return level


def gaussian(key, shape, deviation, limit, cuts=(), held_as=jnp.bfloat16):
    values = jax.random.normal(key, shape, jnp.float32) * deviation
    if len(cuts) > 0:
        values = level_of(key, shape, cuts, -0.22, 0.18) * values
    return jnp.clip(values, min=-limit, max=limit).astype(held_as)


def heavy_noise(stream_key, dims, spread, bound, cuts, heavy, kind=jnp.bfloat16):
    entries = spread * jax.random.normal(stream_key, dims, jnp.float32)
    if cuts:
        entries = entries * level_of(stream_key, dims, cuts, -0.22, 0.18)
    return jnp.clip(strengthened(entries, jax.random.fold_in(stream_key, 3), *heavy), -bound, bound).astype(kind)


def setup_inputs(seed: int = 0, part: int = 0) -> dict:
    keys = jax.random.split(jax.random.key(seed), 8)
    part_splits = jax.random.split(jax.random.fold_in(keys[7], part), 8)
    queries = draw_queries(jax.random.fold_in(jax.random.fold_in(keys[7], part), 71), part)
    newest_key_value = gaussian(part_splits[1], (TOTAL_REQUESTS, 2, KEY_VALUE_HEADS * HEAD_SIZE), 1.0, 6.0, ((0, 4),))
    kv_pages = draw_kv_pages(jax.random.fold_in(jax.random.fold_in(keys[7], part), 71), part)
    fetch_slots = draw_fetch_slots(jax.random.fold_in(jax.random.fold_in(keys[7], part), 71), part)
    block_table = draw_block_table(jax.random.fold_in(jax.random.fold_in(keys[7], part), 71), part)
    prefix_len = place_ends(jax.random.randint(part_splits[5], (TOTAL_REQUESTS,), 2, PAGE_LIST_LENGTH * PAGE_TOKENS + 1), jax.random.fold_in(part_splits[5], 1), 2, PAGE_LIST_LENGTH * PAGE_TOKENS).astype(jnp.int32)
    out_weight = heavy_noise(keys[6], (QUERY_HEADS * HEAD_SIZE, D), (QUERY_HEADS * HEAD_SIZE) ** -0.5, 0.09375, ((0, 4),), (0, 1, 4, 2.0))
    return dict(queries=queries, newest_key_value=newest_key_value, kv_pages=kv_pages, fetch_slots=fetch_slots, block_table=block_table, prefix_len=prefix_len, out_weight=out_weight)


def reference(queries, newest_key_value, kv_pages, fetch_slots, block_table, prefix_len, out_weight):
    group_width = QUERY_HEADS // KEY_VALUE_HEADS
    group_of = (jnp.arange(TOTAL_REQUESTS) // REQ_GRP).astype(jnp.int32)
    page_owner = (block_table // GROUP_PAGE_LIMIT).astype(jnp.int32)
    column = (block_table % GROUP_PAGE_LIMIT).astype(jnp.int32)
    stored = fetch_slots[group_of[:, None], page_owner, column]
    page_index = (page_owner * PAGES_DEV + stored).astype(jnp.int32)
    score_scale = 1.0 / math.sqrt(HEAD_SIZE)

    def single(inputs):
        query_vector, newest_token, pages_used, length = inputs
        chosen_pages = kv_pages[pages_used]
        key_matrix = chosen_pages[:, 0].reshape(PAGE_LIST_LENGTH * PAGE_TOKENS, KEY_VALUE_HEADS, HEAD_SIZE).astype(jnp.float32)
        value_matrix = chosen_pages[:, 1].reshape(PAGE_LIST_LENGTH * PAGE_TOKENS, KEY_VALUE_HEADS, HEAD_SIZE).astype(jnp.float32)
        head_list = query_vector.reshape(KEY_VALUE_HEADS, group_width, HEAD_SIZE).astype(jnp.float32)
        newest_rows = newest_token.reshape(2, KEY_VALUE_HEADS, HEAD_SIZE).astype(jnp.float32)
        scores = jnp.einsum('kqd,pkd->kqp', head_list, key_matrix) * score_scale
        live_mask = jnp.arange(PAGE_LIST_LENGTH * PAGE_TOKENS) < length
        scores = jnp.where(live_mask[None, None, :], scores, -jnp.inf)
        own_score = jnp.einsum('kqd,kd->kq', head_list, newest_rows[0]) * score_scale
        row_top = jnp.maximum(lax.optimization_barrier(jnp.max(scores, axis=-1)), own_score)
        exp_terms = jnp.exp(scores - row_top[..., None])
        exp_own = jnp.exp(own_score - row_top)
        denom_sum = lax.optimization_barrier(jnp.sum(exp_terms, axis=-1)) + exp_own
        weights = (exp_terms / denom_sum[..., None]).astype(jnp.bfloat16).astype(jnp.float32)
        weight_own = (exp_own / denom_sum).astype(jnp.bfloat16).astype(jnp.float32)
        mixed = jnp.einsum('kqp,pkd->kqd', weights, value_matrix)
        mixed = mixed + weight_own[..., None] * newest_rows[1][:, None, :]
        return mixed.astype(jnp.bfloat16).reshape(QUERY_HEADS * HEAD_SIZE)
    mix = lax.map(single, (queries, newest_key_value, page_index, prefix_len))
    return jnp.dot(mix, out_weight, preferred_element_type=jnp.float32).astype(jnp.bfloat16)
```

```python
import functools
import math

import jax
import jax.numpy as jnp
from jax import lax
from jax.experimental import pallas as pl
from jax.experimental.pallas import tpu as pltpu
from jax.sharding import PartitionSpec as P

QUERY_HEADS = 64
KEY_VALUE_HEADS = 8
HEAD_SIZE = 128
GROUP_WIDTH = QUERY_HEADS // KEY_VALUE_HEADS
DEAD = -1e30
SCALE = math.log2(math.e) / math.sqrt(HEAD_SIZE)
MESH = pl.DeviceIdType.MESH
VMEM_LIMIT = 60 * 1024 * 1024

VMEM_SPEC = pl.BlockSpec(memory_space=pltpu.VMEM)
ANY_SPEC = pl.BlockSpec(memory_space=pl.ANY)


def meet(axes):
    barrier = pltpu.get_barrier_semaphore()
    total = 0
    for axis in axes:
        count = lax.axis_size(axis)
        me = lax.axis_index(axis)
        for d in range(1, count):
            pl.semaphore_signal(
                barrier, inc=1, device_id={axis: lax.rem(me + d, count)}, device_id_type=MESH
            )
        total += count - 1
    pl.semaphore_wait(barrier, total)


def spread(axis, source_of, dest_of, send_sem, recv_sem, own_sem):
    count = lax.axis_size(axis)
    me = lax.axis_index(axis)
    copies = []
    for d in range(1, count):
        target = lax.rem(me + d, count)
        copy = pltpu.make_async_remote_copy(
            src_ref=source_of(target),
            dst_ref=dest_of(me),
            send_sem=send_sem.at[d],
            recv_sem=recv_sem.at[d],
            device_id={axis: target},
            device_id_type=MESH,
        )
        copy.start()
        copies.append(copy)
    own = pltpu.make_async_copy(source_of(me), dest_of(me), own_sem)
    own.start()
    copies.append(own)
    return copies


def fetch_kernel(
    heads_dev, width, q_ref, kv_ref, meta_ref, em_ref,
    q_all, pages_all, meta_all, em_all,
    sems_a, sems_b, sems_c, sems_d, sems_e, sems_f, sems_g, sems_h, own_sems,
):
    meet(("tp", "grp"))

    def columns(t):
        first = (t * heads_dev // GROUP_WIDTH) * HEAD_SIZE
        return kv_ref.at[:, :, :, pl.ds(pl.multiple_of(first, HEAD_SIZE), width)]

    copies = spread("tp", columns, lambda t: pages_all.at[t], sems_a, sems_b, own_sems.at[0])
    copies += spread("grp", lambda g: q_ref, lambda g: q_all.at[g], sems_c, sems_d, own_sems.at[1])
    copies += spread("grp", lambda g: meta_ref, lambda g: meta_all.at[g], sems_e, sems_f, own_sems.at[2])
    copies += spread("tp", lambda t: em_ref, lambda t: em_all.at[t], sems_g, sems_h, own_sems.at[3])
    for copy in copies:
        copy.wait()


def attend_kernel(list_len, q_ref, pages_ref, meta_ref, em_ref, o_ref, st_ref, mask_ref):
    groups, rows, cols = q_ref.shape
    owners, per_owner, _, page, width = pages_ref.shape
    heads = cols // HEAD_SIZE
    kv_heads = width // HEAD_SIZE
    per_kv = heads // kv_heads
    tokens = owners * per_owner * page
    lane_j = lax.broadcasted_iota(jnp.int32, (rows, list_len), 1)
    lane_t = lax.broadcasted_iota(jnp.int32, (rows, page), 1)

    def build(step, carry):
        g, t = step // owners, step % owners
        meta = meta_ref[g]
        entries = meta[:, :list_len]
        length = meta[:, list_len : list_len + 1]
        full, tail = length // page, length % page
        matches = em_ref[t, pl.ds(g, 1), :]
        for p in range(per_owner):
            same = entries == matches[:, p : p + 1]
            whole = jnp.sum(jnp.where(same & (lane_j < full), 1.0, 0.0), axis=1, keepdims=True)
            part = jnp.sum(jnp.where(same & (lane_j == full), 1.0, 0.0), axis=1, keepdims=True)
            count = whole + jnp.where(lane_t < tail, part, 0.0)
            start = pl.multiple_of((t * per_owner + p) * page, page)
            mask_ref[pl.ds(pl.multiple_of(g * rows, 8), rows), pl.ds(start, page)] = jnp.where(
                count > 0.0, jnp.log2(jnp.maximum(count, 1.0)), DEAD
            )
        return carry

    lax.fori_loop(0, groups * owners, build, 0)
    st_ref[...] = jnp.zeros(st_ref.shape, jnp.float32)

    g_block = max(1, min(groups, 256 // rows))
    row_block = g_block * rows
    blocks = groups // g_block
    owner_chunk = max(1, min(owners, 2048 // (per_owner * page)))
    chunk = owner_chunk * per_owner * page
    lane_s = lax.broadcasted_iota(jnp.int32, (row_block, st_ref.shape[2]), 1)

    for k in range(kv_heads):
        kv_cols = slice(k * HEAD_SIZE, (k + 1) * HEAD_SIZE)

        def one(step, carry):
            block, head = step // per_kv, k * per_kv + step % per_kv
            g0 = block * g_block
            head_cols = pl.ds(pl.multiple_of(head * HEAD_SIZE, HEAD_SIZE), HEAD_SIZE)
            q = q_ref[pl.ds(g0, g_block), :, head_cols].reshape(row_block, HEAD_SIZE)
            top = None
            for c in range(owners // owner_chunk):
                own = slice(c * owner_chunk, (c + 1) * owner_chunk)
                keys = pages_ref[own, :, 0, :, kv_cols].reshape(chunk, HEAD_SIZE)
                values = pages_ref[own, :, 1, :, kv_cols].reshape(chunk, HEAD_SIZE)
                s = lax.dot_general(
                    q, keys, (((1,), (1,)), ((), ())), preferred_element_type=jnp.float32
                )
                s = s * SCALE + mask_ref[
                    pl.ds(pl.multiple_of(block * row_block, 8), row_block),
                    c * chunk : (c + 1) * chunk,
                ]
                here = jnp.max(s, axis=1, keepdims=True)
                new_top = here if top is None else jnp.maximum(top, here)
                e = jnp.exp2(s - new_top)
                total = jnp.sum(e, axis=1, keepdims=True)
                mixed = jnp.dot(
                    e.astype(jnp.bfloat16), values, preferred_element_type=jnp.float32
                )
                if top is None:
                    denom, acc = total, mixed
                else:
                    fade = jnp.exp2(top - new_top)
                    denom, acc = denom * fade + total, acc * fade + mixed
                top = new_top
            o_ref[pl.ds(g0, g_block), :, head_cols] = acc.astype(jnp.bfloat16).reshape(
                g_block, rows, HEAD_SIZE
            )
            old = st_ref[pl.ds(g0, g_block)].reshape(row_block, st_ref.shape[2])
            new = jnp.where(lane_s == head, top, jnp.where(lane_s == head + heads, denom, old))
            st_ref[pl.ds(g0, g_block)] = new.reshape(g_block, rows, st_ref.shape[2])
            return carry

        lax.fori_loop(0, per_kv * blocks, one, 0)


def return_kernel(o_ref, st_ref, o_all, st_all, sems_a, sems_b, sems_c, sems_d, own_sems):
    meet(("grp",))
    copies = spread("grp", lambda g: o_ref.at[g], lambda g: o_all.at[g], sems_a, sems_b, own_sems.at[0])
    copies += spread("grp", lambda g: st_ref.at[g], lambda g: st_all.at[g], sems_c, sems_d, own_sems.at[1])
    for copy in copies:
        copy.wait()


def merge(q_ref, new_ref, o_all, st_all, mix_ref):
    groups, rows, cols = o_all.shape
    heads = cols // HEAD_SIZE
    per_kv = heads // (new_ref.shape[2] // HEAD_SIZE)
    for h in range(heads):
        k = h // per_kv
        head_cols = slice(h * HEAD_SIZE, (h + 1) * HEAD_SIZE)
        kv_cols = slice(k * HEAD_SIZE, (k + 1) * HEAD_SIZE)
        new_key = new_ref[0, :, kv_cols].astype(jnp.float32)
        new_value = new_ref[1, :, kv_cols].astype(jnp.float32)
        own = jnp.sum(q_ref[:, head_cols].astype(jnp.float32) * new_key, axis=1, keepdims=True) * SCALE
        tops = [st_all[g, :, h : h + 1] for g in range(groups)]
        top = functools.reduce(jnp.maximum, tops, own)
        own = jnp.exp2(own - top)
        denom, acc = own, own * new_value
        for g in range(groups):
            fade = jnp.exp2(tops[g] - top)
            denom = denom + fade * st_all[g, :, heads + h : heads + h + 1]
            acc = acc + fade * o_all[g, :, head_cols].astype(jnp.float32)
        mix_ref[:, head_cols] = (acc / denom).astype(jnp.bfloat16)


def project_kernel(q_ref, new_ref, o_all, st_all, w_ref, out_ref, mix_ref):
    @pl.when(pl.program_id(0) == 0)
    def _():
        merge(q_ref, new_ref, o_all, st_all, mix_ref)

    out_ref[0] = jnp.dot(
        mix_ref[...], w_ref[...], preferred_element_type=jnp.float32
    ).astype(jnp.bfloat16)


def sum_kernel(part_ref, out_ref, parts, sems_a, sems_b, own_sem):
    meet(("tp",))
    copies = spread("tp", lambda t: part_ref.at[t], lambda t: parts.at[t], sems_a, sems_b, own_sem)
    for copy in copies:
        copy.wait()
    total = parts[0].astype(jnp.float32)
    for t in range(1, parts.shape[0]):
        total = total + parts[t].astype(jnp.float32)
    out_ref[...] = total.astype(jnp.bfloat16)


def per_device(
    queries, newest_key_value, kv_pages, fetch_slots, block_table, prefix_len, out_weight
):
    T = lax.axis_size("tp")
    G = lax.axis_size("grp")
    tp_rank = lax.axis_index("tp")
    owner = lax.axis_index("grp") * T + tp_rank
    rows, cols = queries.shape
    heads = cols // HEAD_SIZE
    kv_dev = max(1, heads // GROUP_WIDTH)
    width = kv_dev * HEAD_SIZE
    pages_dev, _, page, _ = kv_pages.shape
    list_len = block_table.shape[1]
    limit = fetch_slots.shape[2]
    model = out_weight.shape[1]
    dma = pltpu.SemaphoreType.DMA

    meta = jnp.concatenate([block_table, prefix_len[:, None]], axis=1)
    meta = jnp.pad(meta, ((0, 0), (0, 128 - list_len - 1)))
    slots = fetch_slots.reshape(G, limit)
    hit = slots[:, None, :] == jnp.arange(pages_dev)[None, :, None]
    entry = owner * limit + jnp.arange(limit, dtype=jnp.int32)
    em = jnp.max(jnp.where(hit, entry[None, None, :], -1), axis=2).astype(jnp.int32)
    g_pad = -(-G // 8) * 8
    em = jnp.pad(em, ((0, g_pad - G), (0, 128 - pages_dev)), constant_values=-1)

    q_all, pages_all, meta_all, em_all = pl.pallas_call(
        functools.partial(fetch_kernel, heads, width),
        out_shape=(
            jax.ShapeDtypeStruct((G, rows, cols), jnp.bfloat16),
            jax.ShapeDtypeStruct((T, pages_dev, 2, page, width), jnp.bfloat16),
            jax.ShapeDtypeStruct((G, rows, 128), jnp.int32),
            jax.ShapeDtypeStruct((T, g_pad, 128), jnp.int32),
        ),
        in_specs=[ANY_SPEC] * 4,
        out_specs=(VMEM_SPEC,) * 4,
        scratch_shapes=[dma((T,)), dma((T,)), dma((G,)), dma((G,)), dma((G,)), dma((G,)), dma((T,)), dma((T,)), dma((4,))],
        compiler_params=pltpu.CompilerParams(
            collective_id=0, has_side_effects=True, vmem_limit_bytes=VMEM_LIMIT
        ),
        name="fetch",
    )(queries, kv_pages, meta, em)

    o_part, st_part = pl.pallas_call(
        functools.partial(attend_kernel, list_len),
        out_shape=(
            jax.ShapeDtypeStruct((G, rows, cols), jnp.bfloat16),
            jax.ShapeDtypeStruct((G, rows, 128), jnp.float32),
        ),
        in_specs=[VMEM_SPEC] * 4,
        out_specs=(VMEM_SPEC,) * 2,
        scratch_shapes=[pltpu.VMEM((G * rows, T * pages_dev * page), jnp.float32)],
        compiler_params=pltpu.CompilerParams(vmem_limit_bytes=VMEM_LIMIT),
        name="attend",
    )(q_all, pages_all, meta_all, em_all)

    o_all, st_all = pl.pallas_call(
        return_kernel,
        out_shape=(
            jax.ShapeDtypeStruct((G, rows, cols), jnp.bfloat16),
            jax.ShapeDtypeStruct((G, rows, 128), jnp.float32),
        ),
        in_specs=[ANY_SPEC] * 2,
        out_specs=(VMEM_SPEC,) * 2,
        scratch_shapes=[dma((G,)), dma((G,)), dma((G,)), dma((G,)), dma((2,))],
        compiler_params=pltpu.CompilerParams(
            collective_id=1, has_side_effects=True, vmem_limit_bytes=VMEM_LIMIT
        ),
        name="give_back",
    )(o_part, st_part)

    kv_first = (tp_rank * heads // GROUP_WIDTH) * HEAD_SIZE
    newest = lax.dynamic_slice_in_dim(newest_key_value, kv_first, width, 2).transpose(1, 0, 2)
    share = model // T
    block = min(1024, share)
    per_share = share // block
    depth = out_weight.shape[0]
    parts = pl.pallas_call(
        project_kernel,
        out_shape=jax.ShapeDtypeStruct((T, rows, share), jnp.bfloat16),
        grid=(model // block,),
        in_specs=[
            pl.BlockSpec((rows, cols), lambda j: (0, 0)),
            pl.BlockSpec((2, rows, width), lambda j: (0, 0, 0)),
            pl.BlockSpec((G, rows, cols), lambda j: (0, 0, 0)),
            pl.BlockSpec((G, rows, 128), lambda j: (0, 0, 0)),
            pl.BlockSpec((depth, block), lambda j: (0, j)),
        ],
        out_specs=pl.BlockSpec((1, rows, block), lambda j: (j // per_share, 0, j % per_share)),
        scratch_shapes=[pltpu.VMEM((rows, cols), jnp.bfloat16)],
        compiler_params=pltpu.CompilerParams(vmem_limit_bytes=VMEM_LIMIT),
        name="project",
    )(queries, newest, o_all, st_all, out_weight)

    return pl.pallas_call(
        sum_kernel,
        out_shape=jax.ShapeDtypeStruct((rows, share), jnp.bfloat16),
        in_specs=[ANY_SPEC],
        out_specs=VMEM_SPEC,
        scratch_shapes=[pltpu.VMEM((T, rows, share), jnp.bfloat16), dma((T,)), dma((T,)), dma],
        compiler_params=pltpu.CompilerParams(
            collective_id=2, has_side_effects=True, vmem_limit_bytes=VMEM_LIMIT
        ),
        name="sum_up",
    )(parts)


def solution(mesh):
    in_specs = (
        P(("rep", "grp"), "tp"),
        P(("rep", "grp"), None, None),
        P(("rep", "grp", "tp"), None, None, None),
        P("rep", ("grp", "tp"), None),
        P(("rep", "grp"), None),
        P(("rep", "grp")),
        P("tp", None),
    )
    out_specs = P(("rep", "grp"), "tp")
    return jax.shard_map(
        per_device, mesh=mesh, in_specs=in_specs, out_specs=out_specs, check_vma=False
    )
```

```python
import functools
import math

import jax
import jax.numpy as jnp
from jax import lax
from jax.experimental import pallas as pl
from jax.experimental.pallas import tpu as pltpu
from jax.sharding import PartitionSpec as P

QUERY_HEADS = 64
KEY_VALUE_HEADS = 8
HEAD_SIZE = 128
GROUP_WIDTH = QUERY_HEADS // KEY_VALUE_HEADS
DEAD = -1e30
SCALE = math.log2(math.e) / math.sqrt(HEAD_SIZE)
MESH = pl.DeviceIdType.MESH
VMEM_LIMIT = 60 * 1024 * 1024

VMEM_SPEC = pl.BlockSpec(memory_space=pltpu.VMEM)
ANY_SPEC = pl.BlockSpec(memory_space=pl.ANY)


def routes(axis):
    count = lax.axis_size(axis)
    me = lax.axis_index(axis)
    if axis == "tp" and count % 2 == 0:
        pair, core = me // 2, me % 2
        pairs = count // 2
        steps = [(i, b) for i in range(1, pairs) for b in range(2)] + [(0, 1)]
        return [lax.rem(pair + i, pairs) * 2 + lax.rem(core + b, 2) for i, b in steps]
    return [lax.rem(me + d, count) for d in range(1, count)]


def meet(axes):
    barrier = pltpu.get_barrier_semaphore()
    total = 0
    for axis in axes:
        for target in routes(axis):
            pl.semaphore_signal(barrier, inc=1, device_id={axis: target}, device_id_type=MESH)
            total += 1
    pl.semaphore_wait(barrier, total)


def remote(source, dest, send_sem, recv_sem, axis, target):
    return pltpu.make_async_remote_copy(
        src_ref=source,
        dst_ref=dest,
        send_sem=send_sem,
        recv_sem=recv_sem,
        device_id={axis: target},
        device_id_type=MESH,
    )


def spread(axis, source_of, dest, send_sem, recv_sem, own_sem):
    me = lax.axis_index(axis)
    copies = []
    for i, target in enumerate(routes(axis)):
        copies.append(
            remote(source_of(target), dest, send_sem.at[i], recv_sem.at[i], axis, target)
        )
    copies.append(pltpu.make_async_copy(source_of(me), dest, own_sem))
    for copy in copies:
        copy.start()
    return copies


def wait_all(copies):
    for copy in copies:
        copy.wait()


def build_mask(list_len, groups, rows, owners, per_owner, page, meta_ref, em_ref, mask_ref):
    lane_j = lax.broadcasted_iota(jnp.int32, (rows, list_len), 1)
    lane_t = lax.broadcasted_iota(jnp.int32, (rows, page), 1)

    def build(step, carry):
        g, t = step // owners, step % owners
        meta = meta_ref[g]
        entries = meta[:, :list_len]
        length = meta[:, list_len : list_len + 1]
        full, tail = length // page, length % page
        matches = em_ref[t, pl.ds(g, 1), :]
        for p in range(per_owner):
            same = entries == matches[:, p : p + 1]
            whole = jnp.sum(jnp.where(same & (lane_j < full), 1.0, 0.0), axis=1, keepdims=True)
            part = jnp.sum(jnp.where(same & (lane_j == full), 1.0, 0.0), axis=1, keepdims=True)
            count = whole + jnp.where(lane_t < tail, part, 0.0)
            start = pl.multiple_of((t * per_owner + p) * page, page)
            mask_ref[pl.ds(pl.multiple_of(g * rows, 8), rows), pl.ds(start, page)] = jnp.where(
                count > 0.0, jnp.log2(jnp.maximum(count, 1.0)), DEAD
            )
        return carry

    lax.fori_loop(0, groups * owners, build, 0)


def merge(q_ref, new_ref, o_parts, st_parts, mix_ref):
    rows, cols = mix_ref.shape
    heads = cols // HEAD_SIZE
    per_kv = heads // (new_ref.shape[2] // HEAD_SIZE)
    for h in range(heads):
        k = h // per_kv
        head_cols = slice(h * HEAD_SIZE, (h + 1) * HEAD_SIZE)
        kv_cols = slice(k * HEAD_SIZE, (k + 1) * HEAD_SIZE)
        new_key = new_ref[0, :, kv_cols].astype(jnp.float32)
        new_value = new_ref[1, :, kv_cols].astype(jnp.float32)
        own = jnp.sum(q_ref[:, head_cols].astype(jnp.float32) * new_key, axis=1, keepdims=True) * SCALE
        tops = [st[:, h : h + 1] for st in st_parts]
        top = functools.reduce(jnp.maximum, tops, own)
        own = jnp.exp2(own - top)
        denom, acc = own, own * new_value
        for part, st, part_top in zip(o_parts, st_parts, tops):
            fade = jnp.exp2(part_top - top)
            denom = denom + fade * st[:, heads + h : heads + h + 1]
            acc = acc + fade * part[:, head_cols].astype(jnp.float32)
        mix_ref[:, head_cols] = (acc / denom).astype(jnp.bfloat16)


def step_kernel(
    list_len, q_in, kv_in, meta_in, em_in, new_ref, w_in, out_ref,
    q_ref, pages_ref, meta_ref, em_ref, mask_ref, o_ref, st_ref, o_got, st_got,
    w_ref, mix_ref, part_ref, part_got, own_part,
    tp_send, tp_recv, grp_send, grp_recv, own_sems, w_sems,
):
    groups, rows, cols = q_ref.shape
    owners, kv_heads, per_owner, _, page, _ = pages_ref.shape
    heads = cols // HEAD_SIZE
    per_kv = heads // kv_heads
    my_group, my_tp = lax.axis_index("grp"), lax.axis_index("tp")
    model = w_in.shape[1]
    share = model // owners

    meet(("tp", "grp"))

    small = spread("tp", lambda t: em_in, em_ref.at[my_tp], tp_send.at[0], tp_recv.at[0], own_sems.at[0])
    small += spread("grp", lambda g: meta_in, meta_ref.at[my_group], grp_send.at[0], grp_recv.at[0], own_sems.at[1])
    arrivals = []
    for k in range(kv_heads):

        def columns(t):
            first = (t * heads // GROUP_WIDTH + k) * HEAD_SIZE
            return kv_in.at[:, :, :, pl.ds(pl.multiple_of(first, HEAD_SIZE), HEAD_SIZE)]

        span = slice(k * per_kv * HEAD_SIZE, (k + 1) * per_kv * HEAD_SIZE)
        n = 1 + k
        copies = spread("tp", columns, pages_ref.at[my_tp, k], tp_send.at[n], tp_recv.at[n], own_sems.at[2 * n])
        copies += spread(
            "grp", lambda g: q_in.at[:, span], q_ref.at[my_group, :, span],
            grp_send.at[n], grp_recv.at[n], own_sems.at[2 * n + 1],
        )
        arrivals.append(copies)

    targets = routes("tp") + [my_tp]
    w_copies = []
    for i, t in enumerate(targets):
        span = pl.ds(pl.multiple_of(t * share, 128), share)
        w_copies.append(pltpu.make_async_copy(w_in.at[:, span], w_ref.at[i], w_sems.at[i]))
        w_copies[-1].start()

    wait_all(small)
    build_mask(list_len, groups, rows, owners, per_owner, page, meta_ref, em_ref, mask_ref)
    st_ref[...] = jnp.zeros(st_ref.shape, jnp.float32)

    g_block = max(1, min(groups, 256 // rows))
    row_block = g_block * rows
    blocks = groups // g_block
    owner_chunk = max(1, min(owners, 2048 // (per_owner * page)))
    chunk = owner_chunk * per_owner * page
    lane_s = lax.broadcasted_iota(jnp.int32, (row_block, st_ref.shape[2]), 1)
    unroll = 2 if per_kv % 2 == 0 else 1
    piece = unroll * HEAD_SIZE
    group_targets = routes("grp")
    o_slot, st_slot = 1 + kv_heads, 2 + kv_heads

    def one(k, block, head):
        g0 = block * g_block
        head_cols = pl.ds(pl.multiple_of(head * HEAD_SIZE, HEAD_SIZE), HEAD_SIZE)
        q = q_ref[pl.ds(g0, g_block), :, head_cols].reshape(row_block, HEAD_SIZE)
        top = None
        for c in range(owners // owner_chunk):
            own = slice(c * owner_chunk, (c + 1) * owner_chunk)
            keys = pages_ref[own, k, :, 0].reshape(chunk, HEAD_SIZE)
            values = pages_ref[own, k, :, 1].reshape(chunk, HEAD_SIZE)
            s = lax.dot_general(
                q, keys, (((1,), (1,)), ((), ())), preferred_element_type=jnp.float32
            )
            s = s * SCALE + mask_ref[
                pl.ds(pl.multiple_of(block * row_block, 8), row_block),
                c * chunk : (c + 1) * chunk,
            ]
            here = jnp.max(s, axis=1, keepdims=True)
            new_top = here if top is None else jnp.maximum(top, here)
            e = jnp.exp2(s - new_top)
            total = jnp.sum(e, axis=1, keepdims=True)
            mixed = jnp.dot(e.astype(jnp.bfloat16), values, preferred_element_type=jnp.float32)
            if top is None:
                denom, acc = total, mixed
            else:
                fade = jnp.exp2(top - new_top)
                denom, acc = denom * fade + total, acc * fade + mixed
            top = new_top
        o_ref[pl.ds(g0, g_block), :, head_cols] = acc.astype(jnp.bfloat16).reshape(
            g_block, rows, HEAD_SIZE
        )
        old = st_ref[pl.ds(g0, g_block)].reshape(row_block, st_ref.shape[2])
        new = jnp.where(lane_s == head, top, jnp.where(lane_s == head + heads, denom, old))
        st_ref[pl.ds(g0, g_block)] = new.reshape(g_block, rows, st_ref.shape[2])

    for k in range(kv_heads):
        wait_all(arrivals[k])

        def some(step, carry):
            head0 = k * per_kv + step * unroll

            def rows_of(block, inner):
                for u in range(unroll):
                    one(k, block, head0 + u)
                return inner

            if blocks == 1:
                rows_of(0, 0)
            else:
                lax.fori_loop(0, blocks, rows_of, 0)
            span = pl.ds(pl.multiple_of(head0 * HEAD_SIZE, HEAD_SIZE), piece)
            for i, g in enumerate(group_targets):
                remote(
                    o_ref.at[g, :, span], o_got.at[i, :, span],
                    grp_send.at[o_slot, i], grp_recv.at[o_slot, i], "grp", g,
                ).start()
            return carry

        lax.fori_loop(0, per_kv // unroll, some, 0)

    stats = []
    for i, g in enumerate(group_targets):
        stats.append(
            remote(
                st_ref.at[g], st_got.at[i],
                grp_send.at[st_slot, i], grp_recv.at[st_slot, i], "grp", g,
            )
        )
        stats[-1].start()
    for i, g in enumerate(group_targets):
        remote(
            o_ref.at[g], o_got.at[i],
            grp_send.at[o_slot, i], grp_recv.at[o_slot, i], "grp", g,
        ).wait()
    wait_all(stats)

    parts = [o_got.at[i] for i in range(groups - 1)] + [o_ref.at[my_group]]
    st_parts = [st_got.at[i] for i in range(groups - 1)] + [st_ref.at[my_group]]
    merge(q_ref.at[my_group], new_ref, parts, st_parts, mix_ref)

    block = min(512, share)
    sent = []
    slot = 1 + kv_heads
    for i, t in enumerate(targets):
        w_copies[i].wait()

        def project(s, carry):
            span = pl.ds(pl.multiple_of(s * block, 128), block)
            made = jnp.dot(mix_ref[...], w_ref[i, :, span], preferred_element_type=jnp.float32)
            if i < owners - 1:
                part_ref[i, :, span] = made.astype(jnp.bfloat16)
            else:
                own_part[:, span] = made
            return carry

        lax.fori_loop(0, share // block, project, 0)
        if i < owners - 1:
            sent.append(
                remote(
                    part_ref.at[i], part_got.at[i],
                    tp_send.at[slot, i], tp_recv.at[slot, i], "tp", t,
                )
            )
            sent[-1].start()
    total = own_part[...]
    for i in reversed(range(owners - 1)):
        sent[i].wait()
        total = total + part_got[i].astype(jnp.float32)
    out_ref[...] = total.astype(jnp.bfloat16)


def per_device(
    queries, newest_key_value, kv_pages, fetch_slots, block_table, prefix_len, out_weight
):
    T = lax.axis_size("tp")
    G = lax.axis_size("grp")
    tp_rank = lax.axis_index("tp")
    owner = lax.axis_index("grp") * T + tp_rank
    rows, cols = queries.shape
    heads = cols // HEAD_SIZE
    kv_dev = max(1, heads // GROUP_WIDTH)
    width = kv_dev * HEAD_SIZE
    pages_dev, _, page, _ = kv_pages.shape
    list_len = block_table.shape[1]
    limit = fetch_slots.shape[2]
    model = out_weight.shape[1]
    dma = pltpu.SemaphoreType.DMA

    meta = jnp.concatenate([block_table, prefix_len[:, None]], axis=1)
    meta = jnp.pad(meta, ((0, 0), (0, 128 - list_len - 1)))
    slots = fetch_slots.reshape(G, limit)
    hit = slots[:, None, :] == jnp.arange(pages_dev)[None, :, None]
    entry = owner * limit + jnp.arange(limit, dtype=jnp.int32)
    em = jnp.max(jnp.where(hit, entry[None, None, :], -1), axis=2).astype(jnp.int32)
    g_pad = -(-G // 8) * 8
    em = jnp.pad(em, ((0, g_pad - G), (0, 128 - pages_dev)), constant_values=-1)

    kv_first = (tp_rank * heads // GROUP_WIDTH) * HEAD_SIZE
    newest = lax.dynamic_slice_in_dim(newest_key_value, kv_first, width, 2).transpose(1, 0, 2)
    share = model // T
    bf16, f32, i32 = jnp.bfloat16, jnp.float32, jnp.int32
    vmem = pltpu.VMEM
    return pl.pallas_call(
        functools.partial(step_kernel, list_len),
        out_shape=jax.ShapeDtypeStruct((rows, share), bf16),
        in_specs=[ANY_SPEC] * 4 + [VMEM_SPEC, ANY_SPEC],
        out_specs=VMEM_SPEC,
        scratch_shapes=[
            vmem((G, rows, cols), bf16),
            vmem((T, kv_dev, pages_dev, 2, page, HEAD_SIZE), bf16),
            vmem((G, rows, 128), i32),
            vmem((T, g_pad, 128), i32),
            vmem((G * rows, T * pages_dev * page), f32),
            vmem((G, rows, cols), bf16),
            vmem((G, rows, 128), f32),
            vmem((G - 1, rows, cols), bf16),
            vmem((G - 1, rows, 128), f32),
            vmem((T, out_weight.shape[0], share), bf16),
            vmem((rows, cols), bf16),
            vmem((T - 1, rows, share), bf16),
            vmem((T - 1, rows, share), bf16),
            vmem((rows, share), f32),
            dma((2 + kv_dev, T - 1)),
            dma((2 + kv_dev, T - 1)),
            dma((3 + kv_dev, G - 1)),
            dma((3 + kv_dev, G - 1)),
            dma((2 + 2 * kv_dev,)),
            dma((T,)),
        ],
        compiler_params=pltpu.CompilerParams(
            collective_id=0, has_side_effects=True, vmem_limit_bytes=VMEM_LIMIT
        ),
        name="decode_step",
    )(queries, kv_pages, meta, em, newest, out_weight)


def solution(mesh):
    in_specs = (
        P(("rep", "grp"), "tp"),
        P(("rep", "grp"), None, None),
        P(("rep", "grp", "tp"), None, None, None),
        P("rep", ("grp", "tp"), None),
        P(("rep", "grp"), None),
        P(("rep", "grp")),
        P("tp", None),
    )
    out_specs = P(("rep", "grp"), "tp")
    return jax.shard_map(
        per_device, mesh=mesh, in_specs=in_specs, out_specs=out_specs, check_vma=False
    )
```

```python
import functools
import math

import jax
import jax.numpy as jnp
from jax import lax
from jax.experimental import pallas as pl
from jax.experimental.pallas import tpu as pltpu
from jax.sharding import PartitionSpec as P

QUERY_HEADS = 64
KEY_VALUE_HEADS = 8
HEAD_SIZE = 128
GROUP_WIDTH = QUERY_HEADS // KEY_VALUE_HEADS
DEAD = -1e30
SCALE = math.log2(math.e) / math.sqrt(HEAD_SIZE)
MESH = pl.DeviceIdType.MESH
VMEM_LIMIT = 60 * 1024 * 1024

VMEM_SPEC = pl.BlockSpec(memory_space=pltpu.VMEM)
ANY_SPEC = pl.BlockSpec(memory_space=pl.ANY)


def routes(axis):
    count = lax.axis_size(axis)
    me = lax.axis_index(axis)
    if axis == "tp" and count % 2 == 0:
        pair, core = me // 2, me % 2
        pairs = count // 2
        steps = [(i, b) for i in range(1, pairs) for b in range(2)] + [(0, 1)]
        return [lax.rem(pair + i, pairs) * 2 + lax.rem(core + b, 2) for i, b in steps]
    return [lax.rem(me + d, count) for d in range(1, count)]


def meet(axes):
    barrier = pltpu.get_barrier_semaphore()
    total = 0
    for axis in axes:
        for target in routes(axis):
            pl.semaphore_signal(barrier, inc=1, device_id={axis: target}, device_id_type=MESH)
            total += 1
    pl.semaphore_wait(barrier, total)


def remote(source, dest, send_sem, recv_sem, axis, target):
    return pltpu.make_async_remote_copy(
        src_ref=source,
        dst_ref=dest,
        send_sem=send_sem,
        recv_sem=recv_sem,
        device_id={axis: target},
        device_id_type=MESH,
    )


def spread(axis, source_of, dest, send_sem, recv_sem, own_sem):
    me = lax.axis_index(axis)
    copies = []
    for i, target in enumerate(routes(axis)):
        copies.append(
            remote(source_of(target), dest, send_sem.at[i], recv_sem.at[i], axis, target)
        )
    copies.append(pltpu.make_async_copy(source_of(me), dest, own_sem))
    for copy in copies:
        copy.start()
    return copies


def wait_all(copies):
    for copy in copies:
        copy.wait()


def build_mask(list_len, groups, rows, owners, per_owner, page, meta_ref, em_ref, mask_ref):
    lane_j = lax.broadcasted_iota(jnp.int32, (rows, list_len), 1)
    lane_t = lax.broadcasted_iota(jnp.int32, (rows, page), 1)

    def build(step, carry):
        g, t = step // owners, step % owners
        meta = meta_ref[g]
        entries = meta[:, :list_len]
        length = meta[:, list_len : list_len + 1]
        full, tail = length // page, length % page
        matches = em_ref[t, pl.ds(g, 1), :]
        for p in range(per_owner):
            same = entries == matches[:, p : p + 1]
            whole = jnp.sum(jnp.where(same & (lane_j < full), 1.0, 0.0), axis=1, keepdims=True)
            part = jnp.sum(jnp.where(same & (lane_j == full), 1.0, 0.0), axis=1, keepdims=True)
            count = whole + jnp.where(lane_t < tail, part, 0.0)
            start = pl.multiple_of((t * per_owner + p) * page, page)
            mask_ref[pl.ds(pl.multiple_of(g * rows, 8), rows), pl.ds(start, page)] = jnp.where(
                count > 0.0, jnp.log2(jnp.maximum(count, 1.0)), DEAD
            )
        return carry

    lax.fori_loop(0, groups * owners, build, 0)


def merge(k, per_kv, q_ref, new_ref, o_parts, st_parts, mix_ref):
    heads = mix_ref.shape[1] // HEAD_SIZE
    for h in range(k * per_kv, (k + 1) * per_kv):
        head_cols = slice(h * HEAD_SIZE, (h + 1) * HEAD_SIZE)
        kv_cols = slice(k * HEAD_SIZE, (k + 1) * HEAD_SIZE)
        new_key = new_ref[0, :, kv_cols].astype(jnp.float32)
        new_value = new_ref[1, :, kv_cols].astype(jnp.float32)
        own = jnp.sum(q_ref[:, head_cols].astype(jnp.float32) * new_key, axis=1, keepdims=True) * SCALE
        tops = [st[:, h : h + 1] for st in st_parts]
        top = functools.reduce(jnp.maximum, tops, own)
        own = jnp.exp2(own - top)
        denom, acc = own, own * new_value
        for part, st, part_top in zip(o_parts, st_parts, tops):
            fade = jnp.exp2(part_top - top)
            denom = denom + fade * st[:, heads + h : heads + h + 1]
            acc = acc + fade * part[:, head_cols].astype(jnp.float32)
        mix_ref[:, head_cols] = (acc / denom).astype(jnp.bfloat16)


def step_kernel(
    list_len, q_in, kv_in, meta_in, em_in, new_ref, w_in, out_ref,
    q_ref, pages_ref, meta_ref, em_ref, mask_ref, o_ref, st_ref, o_got, st_got,
    w_ref, mix_ref, part_ref, part_got, acc_ref,
    tp_send, tp_recv, grp_send, grp_recv, own_sems, w_sems,
):
    groups, rows, cols = q_ref.shape
    owners, kv_heads, per_owner, _, page, _ = pages_ref.shape
    heads = cols // HEAD_SIZE
    per_kv = heads // kv_heads
    my_group, my_tp = lax.axis_index("grp"), lax.axis_index("tp")
    model = w_in.shape[1]
    share = model // owners

    meet(("tp", "grp"))

    small = spread("tp", lambda t: em_in, em_ref.at[my_tp], tp_send.at[0], tp_recv.at[0], own_sems.at[0])
    small += spread("grp", lambda g: meta_in, meta_ref.at[my_group], grp_send.at[0], grp_recv.at[0], own_sems.at[1])
    tp_targets, group_targets = routes("tp"), routes("grp")

    def page_columns(t, k, which):
        first = (t * heads // GROUP_WIDTH + k) * HEAD_SIZE
        return kv_in.at[which, :, :, pl.ds(pl.multiple_of(first, HEAD_SIZE), HEAD_SIZE)]

    def page_copies(k, which):
        return [
            remote(
                page_columns(t, k, which), pages_ref.at[my_tp, k, which],
                tp_send.at[1 + k, i], tp_recv.at[1 + k, i], "tp", t,
            )
            for i, t in enumerate(tp_targets)
        ]

    def query_copies(k):
        span = slice(k * per_kv * HEAD_SIZE, (k + 1) * per_kv * HEAD_SIZE)
        return [
            remote(
                q_in.at[:, span], q_ref.at[my_group, :, span],
                grp_send.at[1 + k, i], grp_recv.at[1 + k, i], "grp", g,
            )
            for i, g in enumerate(group_targets)
        ]

    def own_copies(k):
        span = slice(k * per_kv * HEAD_SIZE, (k + 1) * per_kv * HEAD_SIZE)
        return [
            pltpu.make_async_copy(
                page_columns(my_tp, k, slice(None)), pages_ref.at[my_tp, k], own_sems.at[2 + 2 * k]
            ),
            pltpu.make_async_copy(
                q_in.at[:, span], q_ref.at[my_group, :, span], own_sems.at[3 + 2 * k]
            ),
        ]

    def start_all(copies):
        for copy in copies:
            copy.start()

    @pl.when(my_tp % 2 == 0)
    def _():
        start_all(page_copies(0, slice(None)))
        start_all(query_copies(0))

    @pl.when(my_tp % 2 == 1)
    def _():
        start_all(query_copies(0))
        start_all(page_copies(0, slice(None)))

    for k in range(kv_heads):
        start_all(own_copies(k))
        if k > 0:
            start_all(page_copies(k, pl.ds(0, 1)))
            start_all(query_copies(k))

    targets = tp_targets + [my_tp]
    w_copies = []
    for i, t in enumerate(targets):
        span = pl.ds(pl.multiple_of(t * share, 128), share)
        w_copies.append(pltpu.make_async_copy(w_in.at[:, span], w_ref.at[i], w_sems.at[i]))
        w_copies[-1].start()

    wait_all(small)
    build_mask(list_len, groups, rows, owners, per_owner, page, meta_ref, em_ref, mask_ref)
    st_ref[...] = jnp.zeros(st_ref.shape, jnp.float32)

    g_block = max(1, min(groups, 256 // rows))
    row_block = g_block * rows
    blocks = groups // g_block
    owner_chunk = max(1, min(owners, 2048 // (per_owner * page)))
    chunk = owner_chunk * per_owner * page
    lane_s = lax.broadcasted_iota(jnp.int32, (row_block, st_ref.shape[3]), 1)
    unroll = 2 if per_kv % 2 == 0 else 1
    piece = unroll * HEAD_SIZE
    steps = per_kv // unroll

    def stat_copies(k):
        st_slot = 1 + 2 * kv_heads + k
        return [
            remote(
                st_ref.at[k, g], st_got.at[k, i],
                grp_send.at[st_slot, i], grp_recv.at[st_slot, i], "grp", g,
            )
            for i, g in enumerate(group_targets)
        ]

    def one(k, block, head):
        g0 = block * g_block
        head_cols = pl.ds(pl.multiple_of(head * HEAD_SIZE, HEAD_SIZE), HEAD_SIZE)
        q = q_ref[pl.ds(g0, g_block), :, head_cols].reshape(row_block, HEAD_SIZE)
        top = None
        for c in range(owners // owner_chunk):
            own = slice(c * owner_chunk, (c + 1) * owner_chunk)
            keys = pages_ref[own, k, :, 0].reshape(chunk, HEAD_SIZE)
            values = pages_ref[own, k, :, 1].reshape(chunk, HEAD_SIZE)
            s = lax.dot_general(
                q, keys, (((1,), (1,)), ((), ())), preferred_element_type=jnp.float32
            )
            s = s * SCALE + mask_ref[
                pl.ds(pl.multiple_of(block * row_block, 8), row_block),
                c * chunk : (c + 1) * chunk,
            ]
            here = jnp.max(s, axis=1, keepdims=True)
            new_top = here if top is None else jnp.maximum(top, here)
            e = jnp.exp2(s - new_top)
            total = jnp.sum(e, axis=1, keepdims=True)
            mixed = jnp.dot(e.astype(jnp.bfloat16), values, preferred_element_type=jnp.float32)
            if top is None:
                denom, acc = total, mixed
            else:
                fade = jnp.exp2(top - new_top)
                denom, acc = denom * fade + total, acc * fade + mixed
            top = new_top
        o_ref[pl.ds(g0, g_block), :, head_cols] = acc.astype(jnp.bfloat16).reshape(
            g_block, rows, HEAD_SIZE
        )
        old = st_ref[k, pl.ds(g0, g_block)].reshape(row_block, st_ref.shape[3])
        new = jnp.where(lane_s == head, top, jnp.where(lane_s == head + heads, denom, old))
        st_ref[k, pl.ds(g0, g_block)] = new.reshape(g_block, rows, st_ref.shape[3])

    for k in range(kv_heads):
        wait_all(page_copies(k, slice(None)) + query_copies(k) + own_copies(k))
        o_slot = 1 + kv_heads + k

        def some(step, carry):
            head0 = k * per_kv + step * unroll
            if k + 1 < kv_heads:

                @pl.when(step < per_owner - 1)
                def _():
                    start_all(page_copies(k + 1, pl.ds(step + 1, 1)))


            def rows_of(block, inner):
                for u in range(unroll):
                    one(k, block, head0 + u)
                return inner

            if blocks == 1:
                rows_of(0, 0)
            else:
                lax.fori_loop(0, blocks, rows_of, 0)
            span = pl.ds(pl.multiple_of(head0 * HEAD_SIZE, HEAD_SIZE), piece)
            for i, g in enumerate(group_targets):
                remote(
                    o_ref.at[g, :, span], o_got.at[i, :, span],
                    grp_send.at[o_slot, i], grp_recv.at[o_slot, i], "grp", g,
                ).start()
            return carry

        lax.fori_loop(0, steps, some, 0)
        for p in range(steps + 1, per_owner):
            if k + 1 < kv_heads:
                start_all(page_copies(k + 1, pl.ds(p, 1)))
        start_all(stat_copies(k))

    block = min(512, share)
    sent = []
    slot = 1 + kv_heads
    for k in range(kv_heads):
        span = slice(k * per_kv * HEAD_SIZE, (k + 1) * per_kv * HEAD_SIZE)
        o_slot = 1 + kv_heads + k
        for i, g in enumerate(group_targets):
            remote(
                o_ref.at[g, :, span], o_got.at[i, :, span],
                grp_send.at[o_slot, i], grp_recv.at[o_slot, i], "grp", g,
            ).wait()
        wait_all(stat_copies(k))
        parts = [o_got.at[i] for i in range(groups - 1)] + [o_ref.at[my_group]]
        st_parts = [st_got.at[k, i] for i in range(groups - 1)] + [st_ref.at[k, my_group]]
        merge(k, per_kv, q_ref.at[my_group], new_ref, parts, st_parts, mix_ref)
        last = k == kv_heads - 1
        for i, t in enumerate(targets):
            if k == 0:
                w_copies[i].wait()

            def project(step, carry):
                out = pl.ds(pl.multiple_of(step * block, 128), block)
                made = jnp.dot(
                    mix_ref[:, span], w_ref[i, span, out], preferred_element_type=jnp.float32
                )
                if k > 0:
                    made = made + acc_ref[i, :, out]
                if last and i < owners - 1:
                    part_ref[i, :, out] = made.astype(jnp.bfloat16)
                else:
                    acc_ref[i, :, out] = made
                return carry

            lax.fori_loop(0, share // block, project, 0)
            if last and i < owners - 1:
                sent.append(
                    remote(
                        part_ref.at[i], part_got.at[i],
                        tp_send.at[slot, i], tp_recv.at[slot, i], "tp", t,
                    )
                )
                sent[-1].start()
    total = acc_ref[owners - 1]
    for i in reversed(range(owners - 1)):
        sent[i].wait()
        total = total + part_got[i].astype(jnp.float32)
    out_ref[...] = total.astype(jnp.bfloat16)


def per_device(
    queries, newest_key_value, kv_pages, fetch_slots, block_table, prefix_len, out_weight
):
    T = lax.axis_size("tp")
    G = lax.axis_size("grp")
    tp_rank = lax.axis_index("tp")
    owner = lax.axis_index("grp") * T + tp_rank
    rows, cols = queries.shape
    heads = cols // HEAD_SIZE
    kv_dev = max(1, heads // GROUP_WIDTH)
    width = kv_dev * HEAD_SIZE
    pages_dev, _, page, _ = kv_pages.shape
    list_len = block_table.shape[1]
    limit = fetch_slots.shape[2]
    model = out_weight.shape[1]
    dma = pltpu.SemaphoreType.DMA

    meta = jnp.concatenate([block_table, prefix_len[:, None]], axis=1)
    meta = jnp.pad(meta, ((0, 0), (0, 128 - list_len - 1)))
    slots = fetch_slots.reshape(G, limit)
    hit = slots[:, None, :] == jnp.arange(pages_dev)[None, :, None]
    entry = owner * limit + jnp.arange(limit, dtype=jnp.int32)
    em = jnp.max(jnp.where(hit, entry[None, None, :], -1), axis=2).astype(jnp.int32)
    g_pad = -(-G // 8) * 8
    em = jnp.pad(em, ((0, g_pad - G), (0, 128 - pages_dev)), constant_values=-1)

    kv_first = (tp_rank * heads // GROUP_WIDTH) * HEAD_SIZE
    newest = lax.dynamic_slice_in_dim(newest_key_value, kv_first, width, 2).transpose(1, 0, 2)
    share = model // T
    bf16, f32, i32 = jnp.bfloat16, jnp.float32, jnp.int32
    vmem = pltpu.VMEM
    return pl.pallas_call(
        functools.partial(step_kernel, list_len),
        out_shape=jax.ShapeDtypeStruct((rows, share), bf16),
        in_specs=[ANY_SPEC] * 4 + [VMEM_SPEC, ANY_SPEC],
        out_specs=VMEM_SPEC,
        scratch_shapes=[
            vmem((G, rows, cols), bf16),
            vmem((T, kv_dev, pages_dev, 2, page, HEAD_SIZE), bf16),
            vmem((G, rows, 128), i32),
            vmem((T, g_pad, 128), i32),
            vmem((G * rows, T * pages_dev * page), f32),
            vmem((G, rows, cols), bf16),
            vmem((kv_dev, G, rows, 128), f32),
            vmem((G - 1, rows, cols), bf16),
            vmem((kv_dev, G - 1, rows, 128), f32),
            vmem((T, out_weight.shape[0], share), bf16),
            vmem((rows, cols), bf16),
            vmem((T - 1, rows, share), bf16),
            vmem((T - 1, rows, share), bf16),
            vmem((T, rows, share), f32),
            dma((2 + kv_dev, T - 1)),
            dma((2 + kv_dev, T - 1)),
            dma((1 + 3 * kv_dev, G - 1)),
            dma((1 + 3 * kv_dev, G - 1)),
            dma((2 + 2 * kv_dev,)),
            dma((T,)),
        ],
        compiler_params=pltpu.CompilerParams(
            collective_id=0, has_side_effects=True, vmem_limit_bytes=VMEM_LIMIT
        ),
        name="decode_step",
    )(queries, kv_pages, meta, em, newest, out_weight)


def solution(mesh):
    in_specs = (
        P(("rep", "grp"), "tp"),
        P(("rep", "grp"), None, None),
        P(("rep", "grp", "tp"), None, None, None),
        P("rep", ("grp", "tp"), None),
        P(("rep", "grp"), None),
        P(("rep", "grp")),
        P("tp", None),
    )
    out_specs = P(("rep", "grp"), "tp")
    return jax.shard_map(
        per_device, mesh=mesh, in_specs=in_specs, out_specs=out_specs, check_vma=False
    )
```

```python
import functools
import math

import jax
import jax.numpy as jnp
from jax import lax
from jax.experimental import pallas as pl
from jax.experimental.pallas import tpu as pltpu
from jax.sharding import PartitionSpec as P

QUERY_HEADS = 64
KEY_VALUE_HEADS = 8
HEAD_SIZE = 128
GROUP_WIDTH = QUERY_HEADS // KEY_VALUE_HEADS
DEAD = -1e30
SCALE = math.log2(math.e) / math.sqrt(HEAD_SIZE)
MESH = pl.DeviceIdType.MESH
VMEM_LIMIT = 60 * 1024 * 1024

VMEM_SPEC = pl.BlockSpec(memory_space=pltpu.VMEM)
ANY_SPEC = pl.BlockSpec(memory_space=pl.ANY)


def routes(axis):
    count = lax.axis_size(axis)
    me = lax.axis_index(axis)
    if axis == "tp" and count % 2 == 0:
        pair, core = me // 2, me % 2
        pairs = count // 2
        steps = [(i, b) for i in range(1, pairs) for b in range(2)] + [(0, 1)]
        return [lax.rem(pair + i, pairs) * 2 + lax.rem(core + b, 2) for i, b in steps]
    return [lax.rem(me + d, count) for d in range(1, count)]


def meet(axes):
    barrier = pltpu.get_barrier_semaphore()
    total = 0
    for axis in axes:
        for target in routes(axis):
            pl.semaphore_signal(barrier, inc=1, device_id={axis: target}, device_id_type=MESH)
            total += 1
    pl.semaphore_wait(barrier, total)


def remote(source, dest, send_sem, recv_sem, axis, target):
    return pltpu.make_async_remote_copy(
        src_ref=source,
        dst_ref=dest,
        send_sem=send_sem,
        recv_sem=recv_sem,
        device_id={axis: target},
        device_id_type=MESH,
    )


def spread(axis, source_of, dest, send_sem, recv_sem, own_sem):
    me = lax.axis_index(axis)
    copies = []
    for i, target in enumerate(routes(axis)):
        copies.append(
            remote(source_of(target), dest, send_sem.at[i], recv_sem.at[i], axis, target)
        )
    copies.append(pltpu.make_async_copy(source_of(me), dest, own_sem))
    for copy in copies:
        copy.start()
    return copies


def wait_all(copies):
    for copy in copies:
        copy.wait()


def build_mask(list_len, groups, rows, owners, per_owner, page, meta_ref, em_ref, mask_ref):
    lane_j = lax.broadcasted_iota(jnp.int32, (rows, list_len), 1)
    lane_t = lax.broadcasted_iota(jnp.int32, (rows, page), 1)

    def build(step, carry):
        g, t = step // owners, step % owners
        meta = meta_ref[g]
        entries = meta[:, :list_len]
        length = meta[:, list_len : list_len + 1]
        full, tail = length // page, length % page
        matches = em_ref[t, pl.ds(g, 1), :]
        for p in range(per_owner):
            same = entries == matches[:, p : p + 1]
            whole = jnp.sum(jnp.where(same & (lane_j < full), 1.0, 0.0), axis=1, keepdims=True)
            part = jnp.sum(jnp.where(same & (lane_j == full), 1.0, 0.0), axis=1, keepdims=True)
            count = whole + jnp.where(lane_t < tail, part, 0.0)
            start = pl.multiple_of((t * per_owner + p) * page, page)
            mask_ref[pl.ds(pl.multiple_of(g * rows, 8), rows), pl.ds(start, page)] = jnp.where(
                count > 0.0, jnp.log2(jnp.maximum(count, 1.0)), DEAD
            )
        return carry

    lax.fori_loop(0, groups * owners, build, 0)


def merge(k, per_kv, q_ref, new_ref, o_parts, st_parts, mix_ref):
    heads = mix_ref.shape[1] // HEAD_SIZE
    for h in range(k * per_kv, (k + 1) * per_kv):
        head_cols = slice(h * HEAD_SIZE, (h + 1) * HEAD_SIZE)
        kv_cols = slice(k * HEAD_SIZE, (k + 1) * HEAD_SIZE)
        new_key = new_ref[0, :, kv_cols].astype(jnp.float32)
        new_value = new_ref[1, :, kv_cols].astype(jnp.float32)
        own = jnp.sum(q_ref[:, head_cols].astype(jnp.float32) * new_key, axis=1, keepdims=True) * SCALE
        tops = [st[:, h : h + 1] for st in st_parts]
        top = functools.reduce(jnp.maximum, tops, own)
        own = jnp.exp2(own - top)
        denom, acc = own, own * new_value
        for part, st, part_top in zip(o_parts, st_parts, tops):
            fade = jnp.exp2(part_top - top)
            denom = denom + fade * st[:, heads + h : heads + h + 1]
            acc = acc + fade * part[:, head_cols].astype(jnp.float32)
        mix_ref[:, head_cols] = (acc / denom).astype(jnp.bfloat16)


def step_kernel(
    list_len, q_in, kv_in, meta_in, em_in, new_ref, w_in, out_ref,
    q_ref, pages_ref, meta_ref, em_ref, mask_ref, o_ref, st_ref, o_got, st_got,
    w_ref, mix_ref, part_ref, part_got, acc_ref,
    tp_send, tp_recv, grp_send, grp_recv, own_sems, w_sems,
):
    groups, rows, cols = q_ref.shape
    owners, kv_heads, per_owner, _, page, _ = pages_ref.shape
    heads = cols // HEAD_SIZE
    per_kv = heads // kv_heads
    my_group, my_tp = lax.axis_index("grp"), lax.axis_index("tp")
    model = w_in.shape[1]
    share = model // owners

    meet(("tp", "grp"))

    small = spread("tp", lambda t: em_in, em_ref.at[my_tp], tp_send.at[0], tp_recv.at[0], own_sems.at[0])
    small += spread("grp", lambda g: meta_in, meta_ref.at[my_group], grp_send.at[0], grp_recv.at[0], own_sems.at[1])
    tp_targets, group_targets = routes("tp"), routes("grp")

    def page_columns(t, k, which):
        first = (t * heads // GROUP_WIDTH + k) * HEAD_SIZE
        return kv_in.at[which, :, :, pl.ds(pl.multiple_of(first, HEAD_SIZE), HEAD_SIZE)]

    def page_copies(k, which):
        return [
            remote(
                page_columns(t, k, which), pages_ref.at[my_tp, k, which],
                tp_send.at[1 + k, i], tp_recv.at[1 + k, i], "tp", t,
            )
            for i, t in enumerate(tp_targets)
        ]

    def query_copies(k):
        span = slice(k * per_kv * HEAD_SIZE, (k + 1) * per_kv * HEAD_SIZE)
        return [
            remote(
                q_in.at[:, span], q_ref.at[my_group, :, span],
                grp_send.at[1 + k, i], grp_recv.at[1 + k, i], "grp", g,
            )
            for i, g in enumerate(group_targets)
        ]

    def own_copies(k):
        span = slice(k * per_kv * HEAD_SIZE, (k + 1) * per_kv * HEAD_SIZE)
        return [
            pltpu.make_async_copy(
                page_columns(my_tp, k, slice(None)), pages_ref.at[my_tp, k], own_sems.at[2 + 2 * k]
            ),
            pltpu.make_async_copy(
                q_in.at[:, span], q_ref.at[my_group, :, span], own_sems.at[3 + 2 * k]
            ),
        ]

    def start_all(copies):
        for copy in copies:
            copy.start()

    for k in range(kv_heads):
        start_all(query_copies(k))
        start_all(page_copies(k, slice(None)))
        start_all(own_copies(k))

    targets = tp_targets + [my_tp]
    w_copies = []
    for i, t in enumerate(targets):
        span = pl.ds(pl.multiple_of(t * share, 128), share)
        w_copies.append(pltpu.make_async_copy(w_in.at[:, span], w_ref.at[i], w_sems.at[i]))
        w_copies[-1].start()

    wait_all(small)
    build_mask(list_len, groups, rows, owners, per_owner, page, meta_ref, em_ref, mask_ref)
    st_ref[...] = jnp.zeros(st_ref.shape, jnp.float32)

    g_block = max(1, min(groups, 256 // rows))
    row_block = g_block * rows
    blocks = groups // g_block
    owner_chunk = max(1, min(owners, 2048 // (per_owner * page)))
    chunk = owner_chunk * per_owner * page
    lane_s = lax.broadcasted_iota(jnp.int32, (row_block, st_ref.shape[3]), 1)
    unroll = 2 if per_kv % 2 == 0 else 1
    piece = unroll * HEAD_SIZE
    steps = per_kv // unroll

    def stat_copies(k):
        st_slot = 1 + 2 * kv_heads + k
        return [
            remote(
                st_ref.at[k, g], st_got.at[k, i],
                grp_send.at[st_slot, i], grp_recv.at[st_slot, i], "grp", g,
            )
            for i, g in enumerate(group_targets)
        ]

    def one(k, block, head):
        g0 = block * g_block
        head_cols = pl.ds(pl.multiple_of(head * HEAD_SIZE, HEAD_SIZE), HEAD_SIZE)
        q = q_ref[pl.ds(g0, g_block), :, head_cols].reshape(row_block, HEAD_SIZE)
        top = None
        for c in range(owners // owner_chunk):
            own = slice(c * owner_chunk, (c + 1) * owner_chunk)
            keys = pages_ref[own, k, :, 0].reshape(chunk, HEAD_SIZE)
            values = pages_ref[own, k, :, 1].reshape(chunk, HEAD_SIZE)
            s = lax.dot_general(
                q, keys, (((1,), (1,)), ((), ())), preferred_element_type=jnp.float32
            )
            s = s * SCALE + mask_ref[
                pl.ds(pl.multiple_of(block * row_block, 8), row_block),
                c * chunk : (c + 1) * chunk,
            ]
            here = jnp.max(s, axis=1, keepdims=True)
            new_top = here if top is None else jnp.maximum(top, here)
            e = jnp.exp2(s - new_top)
            total = jnp.sum(e, axis=1, keepdims=True)
            mixed = jnp.dot(e.astype(jnp.bfloat16), values, preferred_element_type=jnp.float32)
            if top is None:
                denom, acc = total, mixed
            else:
                fade = jnp.exp2(top - new_top)
                denom, acc = denom * fade + total, acc * fade + mixed
            top = new_top
        o_ref[pl.ds(g0, g_block), :, head_cols] = acc.astype(jnp.bfloat16).reshape(
            g_block, rows, HEAD_SIZE
        )
        old = st_ref[k, pl.ds(g0, g_block)].reshape(row_block, st_ref.shape[3])
        new = jnp.where(lane_s == head, top, jnp.where(lane_s == head + heads, denom, old))
        st_ref[k, pl.ds(g0, g_block)] = new.reshape(g_block, rows, st_ref.shape[3])

    for k in range(kv_heads):
        wait_all(page_copies(k, slice(None)) + query_copies(k) + own_copies(k))
        o_slot = 1 + kv_heads + k

        def some(step, carry):
            head0 = k * per_kv + step * unroll

            def rows_of(block, inner):
                for u in range(unroll):
                    one(k, block, head0 + u)
                return inner

            if blocks == 1:
                rows_of(0, 0)
            else:
                lax.fori_loop(0, blocks, rows_of, 0)
            span = pl.ds(pl.multiple_of(head0 * HEAD_SIZE, HEAD_SIZE), piece)
            for i, g in enumerate(group_targets):
                remote(
                    o_ref.at[g, :, span], o_got.at[i, :, span],
                    grp_send.at[o_slot, i], grp_recv.at[o_slot, i], "grp", g,
                ).start()
            return carry

        lax.fori_loop(0, steps, some, 0)
        start_all(stat_copies(k))

    block = min(512, share)
    sent = []
    slot = 1 + kv_heads
    for k in range(kv_heads):
        span = slice(k * per_kv * HEAD_SIZE, (k + 1) * per_kv * HEAD_SIZE)
        o_slot = 1 + kv_heads + k
        for i, g in enumerate(group_targets):
            remote(
                o_ref.at[g, :, span], o_got.at[i, :, span],
                grp_send.at[o_slot, i], grp_recv.at[o_slot, i], "grp", g,
            ).wait()
        wait_all(stat_copies(k))
        parts = [o_got.at[i] for i in range(groups - 1)] + [o_ref.at[my_group]]
        st_parts = [st_got.at[k, i] for i in range(groups - 1)] + [st_ref.at[k, my_group]]
        merge(k, per_kv, q_ref.at[my_group], new_ref, parts, st_parts, mix_ref)
        last = k == kv_heads - 1
        for i, t in enumerate(targets):
            if k == 0:
                w_copies[i].wait()

            def project(step, carry):
                out = pl.ds(pl.multiple_of(step * block, 128), block)
                made = jnp.dot(
                    mix_ref[:, span], w_ref[i, span, out], preferred_element_type=jnp.float32
                )
                if k > 0:
                    made = made + acc_ref[i, :, out]
                if last and i < owners - 1:
                    part_ref[i, :, out] = made.astype(jnp.bfloat16)
                else:
                    acc_ref[i, :, out] = made
                return carry

            lax.fori_loop(0, share // block, project, 0)
            if last and i < owners - 1:
                sent.append(
                    remote(
                        part_ref.at[i], part_got.at[i],
                        tp_send.at[slot, i], tp_recv.at[slot, i], "tp", t,
                    )
                )
                sent[-1].start()
    total = acc_ref[owners - 1]
    for i in reversed(range(owners - 1)):
        sent[i].wait()
        total = total + part_got[i].astype(jnp.float32)
    out_ref[...] = total.astype(jnp.bfloat16)


def per_device(
    queries, newest_key_value, kv_pages, fetch_slots, block_table, prefix_len, out_weight
):
    T = lax.axis_size("tp")
    G = lax.axis_size("grp")
    tp_rank = lax.axis_index("tp")
    owner = lax.axis_index("grp") * T + tp_rank
    rows, cols = queries.shape
    heads = cols // HEAD_SIZE
    kv_dev = max(1, heads // GROUP_WIDTH)
    width = kv_dev * HEAD_SIZE
    pages_dev, _, page, _ = kv_pages.shape
    list_len = block_table.shape[1]
    limit = fetch_slots.shape[2]
    model = out_weight.shape[1]
    dma = pltpu.SemaphoreType.DMA

    meta = jnp.concatenate([block_table, prefix_len[:, None]], axis=1)
    meta = jnp.pad(meta, ((0, 0), (0, 128 - list_len - 1)))
    slots = fetch_slots.reshape(G, limit)
    hit = slots[:, None, :] == jnp.arange(pages_dev)[None, :, None]
    entry = owner * limit + jnp.arange(limit, dtype=jnp.int32)
    em = jnp.max(jnp.where(hit, entry[None, None, :], -1), axis=2).astype(jnp.int32)
    g_pad = -(-G // 8) * 8
    em = jnp.pad(em, ((0, g_pad - G), (0, 128 - pages_dev)), constant_values=-1)

    kv_first = (tp_rank * heads // GROUP_WIDTH) * HEAD_SIZE
    newest = lax.dynamic_slice_in_dim(newest_key_value, kv_first, width, 2).transpose(1, 0, 2)
    share = model // T
    bf16, f32, i32 = jnp.bfloat16, jnp.float32, jnp.int32
    vmem = pltpu.VMEM
    return pl.pallas_call(
        functools.partial(step_kernel, list_len),
        out_shape=jax.ShapeDtypeStruct((rows, share), bf16),
        in_specs=[ANY_SPEC] * 4 + [VMEM_SPEC, ANY_SPEC],
        out_specs=VMEM_SPEC,
        scratch_shapes=[
            vmem((G, rows, cols), bf16),
            vmem((T, kv_dev, pages_dev, 2, page, HEAD_SIZE), bf16),
            vmem((G, rows, 128), i32),
            vmem((T, g_pad, 128), i32),
            vmem((G * rows, T * pages_dev * page), f32),
            vmem((G, rows, cols), bf16),
            vmem((kv_dev, G, rows, 128), f32),
            vmem((G - 1, rows, cols), bf16),
            vmem((kv_dev, G - 1, rows, 128), f32),
            vmem((T, out_weight.shape[0], share), bf16),
            vmem((rows, cols), bf16),
            vmem((T - 1, rows, share), bf16),
            vmem((T - 1, rows, share), bf16),
            vmem((T, rows, share), f32),
            dma((2 + kv_dev, T - 1)),
            dma((2 + kv_dev, T - 1)),
            dma((1 + 3 * kv_dev, G - 1)),
            dma((1 + 3 * kv_dev, G - 1)),
            dma((2 + 2 * kv_dev,)),
            dma((T,)),
        ],
        compiler_params=pltpu.CompilerParams(
            collective_id=0, has_side_effects=True, vmem_limit_bytes=VMEM_LIMIT
        ),
        name="decode_step",
    )(queries, kv_pages, meta, em, newest, out_weight)


def solution(mesh):
    in_specs = (
        P(("rep", "grp"), "tp"),
        P(("rep", "grp"), None, None),
        P(("rep", "grp", "tp"), None, None, None),
        P("rep", ("grp", "tp"), None),
        P(("rep", "grp"), None),
        P(("rep", "grp")),
        P("tp", None),
    )
    out_specs = P(("rep", "grp"), "tp")
    return jax.shard_map(
        per_device, mesh=mesh, in_specs=in_specs, out_specs=out_specs, check_vma=False
    )
```
